32 devices in a mesh: keys: 8 (over z, x), heads: 4 (over y, core).
Axes of the slice: x: 2, y: 2, z: 4, core: 2. Of those that a mesh axis runs over, the one named last changes fastest.
Arguments:
- queries: bfloat16 [64, 64, 128], P(None, 'heads'), may hold values from -128 to 128
- keys: bfloat16 [131072, 8, 128], P('keys', 'heads'), may hold values from -4 to 4
- values: bfloat16 [131072, 8, 128], P('keys', 'heads'), may hold values from -6 to 6
- out_weight: bfloat16 [8192, 8192], P('heads', 'keys'), may hold values from -0.0625 to 0.0625
- probe: bfloat16 [8192], P('keys'), may hold values from -6 to 6
- knocked: int32 [64, 16], replicated, may hold values from 0 to 31
Outputs:
- readout: float32 [64, 32], P(None, 'keys')
- picked: float32 [64, 16], replicated
The draws below stay inside these ranges and needn't reach their ends.
All inputs are finite; a program needn't handle non-finite values.
Results may differ from the reference program's by a relative error of at most 0.0003.
Values sent between devices are 32-bit elements; how exact they have to be, the bound alone decides.
A program may use at most 128 MiB of HBM per device.

```python
import jax
import jax.numpy as jnp
from jax import lax

D = 8192
HEADS = 64
KV_HEADS = 8
HD = 128
NQ = 64
BLOCK = 4096
PICK = 16
BLOCKS = 32
CONTEXT = 131072


def masked_plan(key):
    count = max(1, min(3, NQ - 1))
    base = jax.random.fold_in(key, 31)
    askers = jax.random.permutation(jax.random.fold_in(base, 1), NQ - 1)[:count].astype(jnp.int32)
    offsets = jax.random.randint(jax.random.fold_in(base, 2), (count,), 0, NQ - 1 - askers)
    rows = CONTEXT - NQ + askers + 1 + offsets
    groups = jax.random.randint(jax.random.fold_in(base, 3), (count,), 0, KV_HEADS)
    within = jax.random.randint(jax.random.fold_in(base, 4), (count,), 0, HEADS // KV_HEADS)
    vectors = jnp.clip(jax.random.normal(jax.random.fold_in(base, 5), (count, HD), jnp.float32), -3.9, 3.9)
    return (rows, groups, within, askers, vectors)


def draw_keys(key, part):
    field = jnp.clip(jax.random.normal(jax.random.fold_in(key, 11), (CONTEXT, KV_HEADS, HD), jnp.float32), -4.0, 4.0)
    late_rows, late_groups, late_within, late_askers, late_vectors = masked_plan(key)
    field = field.at[late_rows, late_groups].set(late_vectors)
    return field.astype(jnp.bfloat16)


def draw_queries(key, part):
    field = 2.5 * jnp.clip(jax.random.normal(jax.random.fold_in(key, 21), (NQ, HEADS, HD), jnp.float32), -6.0, 6.0)
    late_rows, late_groups, late_within, late_askers, late_vectors = masked_plan(key)
    late_count = late_vectors.shape[0]
    late_strength = jnp.linspace(30.0, 60.0, late_count)
    late_scale = late_strength * HD ** 0.5 / jnp.sum(late_vectors * late_vectors, axis=1)
    late_heads = late_groups * (HEADS // KV_HEADS) + late_within
    field = field.at[late_askers, late_heads].set(late_scale[:, None] * late_vectors)
    field = jnp.clip(field, -128.0, 128.0)
    return field.astype(jnp.bfloat16)


def place_ends(values, own_key, low, largest):
    index_at = [jax.random.randint(jax.random.fold_in(own_key, axis), (), 0, length) for axis, length in enumerate(values.shape)]
    widest = values.shape.index(max(values.shape))
    next_to = index_at[:widest] + [(index_at[widest] + 1) % values.shape[widest]] + index_at[widest + 1:]
    return values.at[tuple(index_at)].set(low).at[tuple(next_to)].set(largest)


def block_levels(key, dims, cuts, low, largest):
    gain = 1.0
    for axis_at, blocks in cuts:
        draws = jax.random.uniform(jax.random.fold_in(jax.random.fold_in(key, 6), axis_at), (blocks,), jnp.float32, low / len(cuts), largest / len(cuts))
        gain = gain * jnp.repeat(jnp.exp(draws), dims[axis_at] // blocks).reshape((-1,) + (1,) * (len(dims) - 1 - axis_at))
    return gain


def gaussian(own_key, shape, scale, limit, cuts=(), held_as=jnp.bfloat16):
    gain = block_levels(own_key, shape, cuts, -0.22, 0.18) if cuts else 1.0
    drawn = jax.random.normal(own_key, shape, jnp.float32) * scale * gain
    return jnp.minimum(jnp.maximum(drawn, -limit), limit).astype(held_as)


def setup_inputs(seed: int = 0) -> dict:
    seeds = jax.random.split(jax.random.key(seed), 7)
    queries = draw_queries(jax.random.fold_in(seeds[6], 71), 0)
    keys = draw_keys(jax.random.fold_in(seeds[6], 71), 0)
    values = gaussian(seeds[2], (CONTEXT, KV_HEADS, HD), 1.0, 6.0, ((0, 8), (1, 4)))
    out_weight = gaussian(seeds[3], (HEADS * HD, D), (HEADS * HD) ** -0.5, 0.0625, ((0, 4), (1, 8)))
    probe = gaussian(seeds[4], (D,), 1.0, 6.0, ((0, 8),))
    knocked = place_ends(jax.random.randint(seeds[5], (NQ, PICK), 0, BLOCKS), jax.random.fold_in(seeds[5], 1), 0, BLOCKS - 1).astype(jnp.int32)
    return {"queries": queries, "keys": keys, "values": values, "out_weight": out_weight, "probe": probe, "knocked": knocked}


NEG = -1e30


def combine(first, second):
    m1, s1, o1 = first
    m2, s2, o2 = second
    top = jnp.maximum(m1, m2)
    a = jnp.exp(m1 - top)
    b = jnp.exp(m2 - top)
    return top, s1 * a + s2 * b, o1 * a[..., None] + o2 * b[..., None]


def reference(queries, keys, values, out_weight, probe, knocked):
    group = HEADS // KV_HEADS
    direction = jnp.dot(out_weight, probe, preferred_element_type=jnp.float32).reshape(KV_HEADS, group, HD)
    grouped = queries.astype(jnp.float32).reshape(NQ, KV_HEADS, group, HD)
    key_blocks = keys.reshape(BLOCKS, BLOCK, KV_HEADS, HD)
    value_blocks = values.reshape(BLOCKS, BLOCK, KV_HEADS, HD)
    query_pos = CONTEXT - NQ + jnp.arange(NQ, dtype=jnp.int32)

    def block_state(index):
        kblk = lax.dynamic_index_in_dim(key_blocks, index, 0, False).astype(jnp.float32)
        vblk = lax.dynamic_index_in_dim(value_blocks, index, 0, False).astype(jnp.float32)
        scores = jnp.einsum("qgrd,kgd->qgrk", grouped, kblk) * (HD ** -0.5)
        key_pos = index * BLOCK + jnp.arange(BLOCK, dtype=jnp.int32)
        allowed = key_pos[None, :] <= query_pos[:, None]
        scores = jnp.where(allowed[:, None, None, :], scores, NEG)
        top = jnp.max(scores, axis=-1)
        weights = jnp.exp(scores - top[..., None])
        total = jnp.sum(weights, axis=-1)
        summed = jnp.einsum("qgrk,kgd->qgrd", weights.astype(jnp.bfloat16).astype(jnp.float32), vblk)
        return top, total, summed

    states = lax.map(block_state, jnp.arange(BLOCKS, dtype=jnp.int32))
    empty = (jnp.full((NQ, KV_HEADS, group), NEG, jnp.float32),
             jnp.zeros((NQ, KV_HEADS, group), jnp.float32),
             jnp.zeros((NQ, KV_HEADS, group, HD), jnp.float32))

    def forward(carry, item):
        return combine(carry, item), carry

    _, before = lax.scan(forward, empty, states)
    _, after = lax.scan(forward, empty, states, reverse=True)
    top, total, summed = combine(before, after)
    projected = jnp.sum(summed * direction, axis=-1)
    readout = jnp.sum(projected / total, axis=(2, 3)).T
    picked = jnp.take_along_axis(readout, knocked, axis=1)
    return readout, picked
```

```python
import functools
import math

import jax
import jax.numpy as jnp
from jax import lax
from jax.experimental import pallas as pl
from jax.experimental.pallas import tpu as pltpu
from jax.sharding import PartitionSpec as P

BLOCK = 4096
NEG = -1e30
LANES = 128
SUBL = 8
PIECE = 2048
STEP = 512
MESH = pl.DeviceIdType.MESH
F32 = jnp.float32
BF16 = jnp.bfloat16


def exchange(size, axis, src, dst, send, recv):
    me = lax.axis_index(axis)
    out = []
    for k in range(1, size):
        there = lax.rem(me + k, size)
        here = lax.rem(me + size - k, size)
        put = pltpu.make_async_remote_copy(src, dst(me), send(k), recv(k), device_id={axis: there}, device_id_type=MESH)
        get = pltpu.make_async_remote_copy(src, dst(here), send(k), recv(k), device_id={axis: there}, device_id_type=MESH)
        out.append((put, get))
    return out


def begin(copies):
    for put, _ in copies:
        put.start()


def finish(copies):
    for _, get in copies:
        get.wait_recv()
    for put, _ in copies:
        put.wait_send()


def halves(x, parts):
    out = []
    for _ in range(parts - 1):
        out.append(x.astype(BF16))
        x = x - out[-1].astype(F32)
    out.append(x.astype(BF16))
    return out


def attend(lanes, hn, nblk, kvh, group, q_hbm, k_hbm, v_hbm, w_hbm, x_hbm, n_hbm, read_ref, pick_ref,
           q_v, k_v, v_v, w_v, x_v, n_v, qf, qt, rel, sc, dcat, part, dirs, tots, xs, own, reads, table,
           q_s, k_s, v_s, w_s, x_s, n_s, d_send, d_recv, t_send, t_recv, r_send, r_recv):
    nq, hq, hd = q_hbm.shape
    rows = nq * group
    flat = rows // LANES
    per = LANES // nq
    wide = BLOCK * kvh
    piece = min(PIECE, wide)
    blocks = lanes * nblk
    scale = hd ** -0.5 * math.log2(math.e)
    device = lax.axis_index("keys")
    mine = lax.axis_index("heads")
    barrier = pltpu.get_barrier_semaphore()
    for k in range(1, lanes):
        pl.semaphore_signal(barrier, inc=1, device_id={"keys": lax.rem(device + k, lanes)}, device_id_type=MESH)
    for k in range(1, hn):
        pl.semaphore_signal(barrier, inc=1, device_id={"heads": lax.rem(mine + k, hn)}, device_id_type=MESH)

    def part_of(i):
        return pl.ds(pl.multiple_of(i * wide, wide), wide)

    def fetch_k(i):
        return pltpu.make_async_copy(k_hbm.at[part_of(i)], k_v.at[part_of(i)], k_s.at[i])

    def fetch_v(i):
        return pltpu.make_async_copy(v_hbm.at[part_of(i)], v_v.at[part_of(i)], v_s.at[i])

    fetch_q = pltpu.make_async_copy(q_hbm, q_v, q_s)
    fetch_w = pltpu.make_async_copy(w_hbm, w_v, w_s)
    fetch_x = pltpu.make_async_copy(x_hbm, x_v, x_s)
    fetch_n = pltpu.make_async_copy(n_hbm, n_v, n_s)
    fetch_q.start()
    fetch_x.start()
    fetch_w.start()
    fetch_k(0).start()
    fetch_n.start()
    fetch_v(0).start()
    for i in range(1, nblk):
        fetch_k(i).start()
        fetch_v(i).start()

    tail = nq * kvh
    r = lax.broadcasted_iota(jnp.int32, (tail, rows), 0)
    c = lax.broadcasted_iota(jnp.int32, (tail, rows), 1)
    rel[...] = r // kvh + (BLOCK - nq) - lax.rem(c, nq)
    fetch_q.wait()
    qf[...] = q_v[...].astype(F32).reshape(nq * hq, hd)
    for h in range(kvh):
        for a in range(flat):
            x = jnp.concatenate([qf[pl.ds(h * group + a * per + e, nq, stride=hq), :] for e in range(per)], axis=0)
            qt[h * hd:(h + 1) * hd, a * LANES:(a + 1) * LANES] = x.T.astype(BF16)

    fetch_x.wait()
    x = x_v[...]
    x = jnp.concatenate([x[k:k + 1, :] for k in range(x.shape[0])], axis=1)
    fetch_w.wait()
    some = lax.dot_general(jnp.broadcast_to(x, (16, x.shape[1])), w_v[...], (((1,), (1,)), ((), ())), preferred_element_type=F32)
    for h in range(hq):
        part[h:h + 1, :] = some[0:1, h * hd:(h + 1) * hd]
    pl.semaphore_wait(barrier, lanes + hn - 2)
    send_dirs = exchange(lanes, "keys", part, lambda d: dirs.at[d], lambda k: d_send.at[k], lambda k: d_recv.at[k])
    begin(send_dirs)
    dirs[device] = part[...]

    def states(i):
        return exchange(lanes, "keys", tots.at[device, i], lambda d: tots.at[d, i],
                        lambda k: t_send.at[i, k], lambda k: t_recv.at[i, k])

    odd = lax.broadcasted_iota(jnp.int32, (16, hd), 0)
    pm = [jnp.where(lax.rem(odd, kvh) == h, 1.0, 0.0).astype(BF16)[None] for h in range(kvh)]
    u_row = lax.broadcasted_iota(jnp.int32, (hq, piece), 0)
    u_col = lax.broadcasted_iota(jnp.int32, (hq, piece), 1)
    lane = lax.broadcasted_iota(jnp.int32, (1, LANES), 1)

    def over(op, x):
        step = kvh
        while step < SUBL:
            x = op(x, pltpu.roll(x, step, 0))
            step *= 2
        return x

    @pl.loop(0, nblk)
    def _(i):
        fetch_k(i).wait()
        base = (device * nblk + i) * BLOCK
        first = lanes * nblk * BLOCK - nq
        m = jnp.full((SUBL, rows), 2 * NEG, F32)
        for t in range(wide // piece):
            x = k_v[pl.ds(pl.multiple_of(i * wide + t * piece, piece), piece), :].reshape(piece // 16, 16, hd)
            left = jnp.concatenate([(x * pm[h]).reshape(piece, hd) for h in range(kvh)], axis=1)
            s = jnp.dot(left, qt[...], preferred_element_type=F32) * scale
            if t == wide // piece - 1:
                last = jnp.where(rel[...] <= first - base, s[piece - tail:], NEG)
                s = jnp.concatenate([s[:piece - tail], last], axis=0)
            sc[t] = s
            m = jnp.maximum(m, jnp.max(s.reshape(piece // SUBL, SUBL, rows), axis=0))
        m = over(jnp.maximum, m)

        @pl.when(i == 0)
        def _():
            finish(send_dirs)
            direction = dirs[0]
            for k in range(1, lanes):
                direction = direction + dirs[k]
            dcat[...] = jnp.concatenate(halves(direction, 3), axis=0)

        fetch_v(i).wait()
        l = jnp.zeros((SUBL, rows), F32)
        acc = jnp.zeros((2 * hq, rows), F32)
        for t in range(wide // piece):
            x = v_v[pl.ds(pl.multiple_of(i * wide + t * piece, piece), piece), :]
            u = lax.dot_general(dcat[...], x, (((1,), (1,)), ((), ())), preferred_element_type=F32)
            u = u[0:hq] + u[hq:2 * hq] + u[2 * hq:3 * hq]
            u = jnp.where(lax.rem(u_col, kvh) == u_row // group, u, 0.0)
            left = jnp.concatenate(halves(u, 2), axis=0)
            for g in range(piece // STEP):
                s = sc[t, g * STEP:(g + 1) * STEP, :]
                p = jnp.exp2(s.reshape(STEP // SUBL, SUBL, rows) - m[None])
                l = l + jnp.sum(p, axis=0)
                p = p.reshape(STEP, rows).astype(BF16)
                acc = acc + jnp.dot(left[:, g * STEP:(g + 1) * STEP], p, preferred_element_type=F32)
        l = over(jnp.add, l)
        acc = acc[0:hq] + acc[hq:2 * hq]
        for h in range(kvh):
            for a in range(flat):
                at = slice(a * LANES, (a + 1) * LANES)
                row = pl.ds(h * flat + a, 1)
                tots[device, i, 0, row, :] = m[h:h + 1, at]
                tots[device, i, 1, row, :] = l[h:h + 1, at]
                o = acc[h * group + a * per:h * group + a * per + 1, at]
                for e in range(1, per):
                    g = h * group + a * per + e
                    o = jnp.where(lane // nq == e, acc[g:g + 1, at], o)
                tots[device, i, 2, row, :] = o
        begin(states(i))

    for i in range(nblk):
        finish(states(i))

    ms = [tots[b // nblk, b % nblk, 0] for b in range(blocks)]
    before, after = [ms[0]], [ms[-1]]
    for b in range(1, blocks):
        before.append(jnp.maximum(before[-1], ms[b]))
        after.append(jnp.maximum(after[-1], ms[blocks - 1 - b]))
    after = after[::-1]
    empty = jnp.full_like(ms[0], NEG)
    rest = [jnp.maximum(before[b - 1] if b else empty, after[b + 1] if b < blocks - 1 else empty) for b in range(blocks)]
    top = before[-1]
    second = functools.reduce(jnp.minimum, rest)
    ss, os, s2, o2 = [], [], jnp.zeros_like(top), jnp.zeros_like(top)
    for b in range(blocks):
        s = tots[b // nblk, b % nblk, 1]
        o = tots[b // nblk, b % nblk, 2]
        e = jnp.exp2(ms[b] - top)
        ss.append(s * e)
        os.append(o * e)
        e = jnp.where(ms[b] > second, 0.0, jnp.exp2(ms[b] - second))
        s2 = s2 + s * e
        o2 = o2 + o * e
    alone = o2 / s2

    def others(xs):
        fore, back = [jnp.zeros_like(top)], [jnp.zeros_like(top)]
        for b in range(blocks - 1):
            fore.append(fore[-1] + xs[b])
            back.append(back[-1] + xs[blocks - 1 - b])
        back = back[::-1]
        return [fore[b] + back[b] for b in range(blocks)]

    ss, os = others(ss), others(os)
    states_rows = kvh * flat
    for b in range(blocks):
        xs[b * states_rows:(b + 1) * states_rows, :] = jnp.where(ms[b] > second, alone, os[b] / ss[b])
    x = xs[pl.ds(0, blocks, stride=states_rows), :]
    for j in range(1, states_rows):
        x = x + xs[pl.ds(j, blocks, stride=states_rows), :]
    step = nq
    while step < LANES:
        x = x + pltpu.roll(x, step, 1)
        step *= 2
    own[...] = x
    copies = exchange(hn, "heads", own, lambda d: reads.at[d], lambda k: r_send.at[k], lambda k: r_recv.at[k])
    begin(copies)
    reads[mine] = x
    fetch_n.wait()
    finish(copies)
    x = reads[0]
    for k in range(1, hn):
        x = x + reads[k]
    table[...] = x
    read_ref[...] = table[pl.ds(device * nblk, nblk), 0:nq]
    ids = n_v[...]
    picked = jnp.zeros(ids.shape, F32)
    for b in range(blocks):
        picked = jnp.where(ids == b, x[b:b + 1, 0:nq], picked)
    pick_ref[...] = picked


def body(queries, keys, values, out_weight, probe, knocked):
    nq, hq, hd = queries.shape
    kvh = keys.shape[1]
    group = hq // kvh
    nblk = keys.shape[0] // BLOCK
    lanes = lax.axis_size("keys")
    hn = lax.axis_size("heads")
    rows = nq * group
    flat = rows // LANES
    wide = BLOCK * kvh
    piece = min(PIECE, wide)
    blocks = lanes * nblk
    picks = knocked.shape[1]
    dma = pltpu.SemaphoreType.DMA
    vmem = pltpu.VMEM
    hbm = pl.BlockSpec(memory_space=pl.ANY)
    kernel = pl.pallas_call(
        functools.partial(attend, lanes, hn, nblk, kvh, group),
        in_specs=[hbm] * 6,
        out_specs=[pl.BlockSpec(memory_space=pltpu.VMEM)] * 2,
        out_shape=[jax.ShapeDtypeStruct((nblk, nq), F32), jax.ShapeDtypeStruct((picks, nq), F32)],
        scratch_shapes=[
            vmem((nq, hq, hd), BF16),
            vmem((nblk * wide, hd), BF16),
            vmem((nblk * wide, hd), BF16),
            vmem(out_weight.shape, BF16),
            vmem((probe.shape[0] // LANES, LANES), BF16),
            vmem((picks, nq), jnp.int32),
            vmem((nq * hq, hd), F32),
            vmem((kvh * hd, rows), BF16),
            vmem((nq * kvh, rows), jnp.int32),
            vmem((wide // piece, piece, rows), F32),
            vmem((3 * hq, hd), BF16),
            vmem((hq, hd), F32),
            vmem((lanes, hq, hd), F32),
            vmem((lanes, nblk, 3, kvh * flat, LANES), F32),
            vmem((blocks * kvh * flat, LANES), F32),
            vmem((blocks, LANES), F32),
            vmem((hn, blocks, LANES), F32),
            vmem((blocks, LANES), F32),
            dma, dma((nblk,)), dma((nblk,)), dma, dma, dma,
            dma((lanes,)), dma((lanes,)), dma((nblk, lanes)), dma((nblk, lanes)), dma((hn,)), dma((hn,)),
        ],
        compiler_params=pltpu.CompilerParams(collective_id=0, has_side_effects=True, vmem_limit_bytes=60 * 2 ** 20),
    )
    readout, picked = kernel(queries, keys.reshape(-1, hd), values.reshape(-1, hd), out_weight,
                             probe.reshape(-1, LANES), knocked.T)
    return (readout.T, picked.T)


def solution(mesh):
    in_specs = (
        P(None, "heads", None),
        P("keys", "heads", None),
        P("keys", "heads", None),
        P("heads", "keys"),
        P("keys"),
        P(),
    )
    out_specs = (P(None, "keys"), P())
    return jax.shard_map(body, mesh=mesh, in_specs=in_specs, out_specs=out_specs, check_vma=False)
```

```python
import functools
import math

import jax
import jax.numpy as jnp
from jax import lax
from jax.experimental import pallas as pl
from jax.experimental.pallas import tpu as pltpu
from jax.sharding import PartitionSpec as P

BLOCK = 4096
NEG = -1e30
LANES = 128
SUBL = 8
PIECE = 2048
STEP = 256
AHEAD = 2
MESH = pl.DeviceIdType.MESH
F32 = jnp.float32
BF16 = jnp.bfloat16


def exchange(size, axis, src, dst, send, recv):
    me = lax.axis_index(axis)
    out = []
    for k in range(1, size):
        there = lax.rem(me + k, size)
        here = lax.rem(me + size - k, size)
        put = pltpu.make_async_remote_copy(src, dst(me), send(k), recv(k), device_id={axis: there}, device_id_type=MESH)
        get = pltpu.make_async_remote_copy(src, dst(here), send(k), recv(k), device_id={axis: there}, device_id_type=MESH)
        out.append((put, get))
    return out


def begin(copies):
    for put, _ in copies:
        put.start()


def finish(copies):
    for _, get in copies:
        get.wait_recv()
    for put, _ in copies:
        put.wait_send()


def halves(x, parts):
    out = []
    for _ in range(parts - 1):
        out.append(x.astype(BF16))
        x = x - out[-1].astype(F32)
    out.append(x.astype(BF16))
    return out


def attend(lanes, hn, nblk, kvh, group, q_hbm, k_hbm, v_hbm, w_hbm, x_hbm, n_hbm, read_ref, pick_ref,
           q_v, k_v, v_v, w_v, x_v, n_v, qf, qt, rel, sc, tops, dcat, part, dirs, tots, xs, own, reads, table,
           q_s, k_s, v_s, w_s, x_s, n_s, d_send, d_recv, t_send, t_recv, r_send, r_recv):
    nq, hq, hd = q_hbm.shape
    rows = nq * group
    flat = rows // LANES
    per = LANES // nq
    wide = BLOCK * kvh
    piece = min(PIECE, wide)
    blocks = lanes * nblk
    scale = hd ** -0.5 * math.log2(math.e)
    device = lax.axis_index("keys")
    mine = lax.axis_index("heads")
    barrier = pltpu.get_barrier_semaphore()
    for k in range(1, lanes):
        pl.semaphore_signal(barrier, inc=1, device_id={"keys": lax.rem(device + k, lanes)}, device_id_type=MESH)
    for k in range(1, hn):
        pl.semaphore_signal(barrier, inc=1, device_id={"heads": lax.rem(mine + k, hn)}, device_id_type=MESH)

    def part_of(i):
        return pl.ds(pl.multiple_of(i * wide, wide), wide)

    def fetch_k(i):
        return pltpu.make_async_copy(k_hbm.at[part_of(i)], k_v.at[part_of(i)], k_s.at[i])

    def fetch_v(i):
        return pltpu.make_async_copy(v_hbm.at[part_of(i)], v_v.at[part_of(i)], v_s.at[i])

    fetch_q = pltpu.make_async_copy(q_hbm, q_v, q_s)
    fetch_w = pltpu.make_async_copy(w_hbm, w_v, w_s)
    fetch_x = pltpu.make_async_copy(x_hbm, x_v, x_s)
    fetch_n = pltpu.make_async_copy(n_hbm, n_v, n_s)
    fetch_q.start()
    fetch_x.start()
    fetch_w.start()
    fetch_k(0).start()

    tail = nq * kvh
    r = lax.broadcasted_iota(jnp.int32, (tail, rows), 0)
    c = lax.broadcasted_iota(jnp.int32, (tail, rows), 1)
    rel[...] = r // kvh + (BLOCK - nq) - lax.rem(c, nq)
    fetch_q.wait()
    qf[...] = q_v[...].astype(F32).reshape(nq * hq, hd)
    for h in range(kvh):
        for a in range(flat):
            x = jnp.concatenate([qf[pl.ds(h * group + a * per + e, nq, stride=hq), :] for e in range(per)], axis=0)
            qt[h * hd:(h + 1) * hd, a * LANES:(a + 1) * LANES] = x.T.astype(BF16)

    fetch_x.wait()
    x = x_v[...]
    x = jnp.concatenate([x[k:k + 1, :] for k in range(x.shape[0])], axis=1)
    fetch_w.wait()
    for i in range(1, min(2, nblk)):
        fetch_k(i).start()
    fetch_v(0).start()
    for i in range(1, nblk):
        if i > 1:
            fetch_k(i).start()
        fetch_v(i).start()
    fetch_n.start()
    some = lax.dot_general(jnp.broadcast_to(x, (16, x.shape[1])), w_v[...], (((1,), (1,)), ((), ())), preferred_element_type=F32)
    for h in range(hq):
        part[h:h + 1, :] = some[0:1, h * hd:(h + 1) * hd]
    send_dirs = exchange(lanes, "keys", part, lambda d: dirs.at[d], lambda k: d_send.at[k], lambda k: d_recv.at[k])
    dirs[device] = part[...]

    def states(i):
        return exchange(lanes, "keys", tots.at[device, i], lambda d: tots.at[d, i],
                        lambda k: t_send.at[i, k], lambda k: t_recv.at[i, k])

    odd = lax.broadcasted_iota(jnp.int32, (16, hd), 0)
    pm = [jnp.where(lax.rem(odd, kvh) == h, 1.0, 0.0).astype(BF16)[None] for h in range(kvh)]
    u_row = lax.broadcasted_iota(jnp.int32, (hq, STEP), 0)
    u_col = lax.broadcasted_iota(jnp.int32, (hq, STEP), 1)
    keep = lax.rem(u_col, kvh) == u_row // group
    lane = lax.broadcasted_iota(jnp.int32, (1, LANES), 1)

    def over(op, x):
        step = kvh
        while step < SUBL:
            x = op(x, pltpu.roll(x, step, 0))
            step *= 2
        return x

    def score(i, pieces, m):
        slot = lax.rem(i, 2)
        base = (device * nblk + i) * BLOCK
        first = lanes * nblk * BLOCK - nq
        for t in pieces:
            x = k_v[pl.ds(pl.multiple_of(i * wide + t * piece, piece), piece), :].reshape(piece // 16, 16, hd)
            left = jnp.concatenate([(x * pm[h]).reshape(piece, hd) for h in range(kvh)], axis=1)
            s = jnp.dot(left, qt[...], preferred_element_type=F32) * scale
            if t == wide // piece - 1:
                last = jnp.where(rel[...] <= first - base, s[piece - tail:], NEG)
                s = jnp.concatenate([s[:piece - tail], last], axis=0)
            sc[slot, t] = s
            m = jnp.maximum(m, jnp.max(s.reshape(piece // SUBL, SUBL, rows), axis=0))
        return m

    def project(i, j):
        x = v_v[pl.ds(pl.multiple_of(i * wide + j * STEP, STEP), STEP), :]
        u = lax.dot_general(dcat[...], x, (((1,), (1,)), ((), ())), preferred_element_type=F32)
        u = jnp.where(keep, u[0:hq] + u[hq:2 * hq] + u[2 * hq:3 * hq], 0.0)
        return jnp.concatenate(halves(u, 2), axis=0)

    count = wide // piece
    low = jnp.full((SUBL, rows), 2 * NEG, F32)
    fetch_k(0).wait()
    m = score(0, range(count // 2), low)
    pl.semaphore_wait(barrier, lanes + hn - 2)
    begin(send_dirs)
    tops[0] = over(jnp.maximum, score(0, range(count // 2, count), m))

    @pl.loop(0, nblk)
    def _(i):
        @pl.when(i < nblk - 1)
        def _():
            fetch_k(i + 1).wait()
            tops[lax.rem(i + 1, 2)] = over(jnp.maximum, score(i + 1, range(count), low))

        @pl.when(i == 0)
        def _():
            finish(send_dirs)
            direction = dirs[0]
            for k in range(1, lanes):
                direction = direction + dirs[k]
            dcat[...] = jnp.concatenate(halves(direction, 3), axis=0)

        fetch_v(i).wait()
        slot = lax.rem(i, 2)
        m = tops[slot]
        l = jnp.zeros((SUBL, rows), F32)
        acc = jnp.zeros((2 * hq, rows), F32)
        left = [project(i, j) for j in range(AHEAD)]
        for j in range(wide // STEP):
            if j + AHEAD < wide // STEP:
                left.append(project(i, j + AHEAD))
            t, g = divmod(j * STEP, piece)
            s = sc[slot, t, g:g + STEP, :]
            p = jnp.exp2(s.reshape(STEP // SUBL, SUBL, rows) - m[None])
            l = l + jnp.sum(p, axis=0)
            acc = acc + jnp.dot(left[j], p.reshape(STEP, rows).astype(BF16), preferred_element_type=F32)
        l = over(jnp.add, l)
        acc = acc[0:hq] + acc[hq:2 * hq]
        for h in range(kvh):
            for a in range(flat):
                at = slice(a * LANES, (a + 1) * LANES)
                row = pl.ds(h * flat + a, 1)
                tots[device, i, 0, row, :] = m[h:h + 1, at]
                tots[device, i, 1, row, :] = l[h:h + 1, at]
                o = acc[h * group + a * per:h * group + a * per + 1, at]
                for e in range(1, per):
                    g = h * group + a * per + e
                    o = jnp.where(lane // nq == e, acc[g:g + 1, at], o)
                tots[device, i, 2, row, :] = o
        begin(states(i))

    for i in range(nblk):
        finish(states(i))

    ms = [tots[b // nblk, b % nblk, 0] for b in range(blocks)]
    before, after = [ms[0]], [ms[-1]]
    for b in range(1, blocks):
        before.append(jnp.maximum(before[-1], ms[b]))
        after.append(jnp.maximum(after[-1], ms[blocks - 1 - b]))
    after = after[::-1]
    empty = jnp.full_like(ms[0], NEG)
    rest = [jnp.maximum(before[b - 1] if b else empty, after[b + 1] if b < blocks - 1 else empty) for b in range(blocks)]
    top = before[-1]
    second = functools.reduce(jnp.minimum, rest)
    ss, os, s2, o2 = [], [], jnp.zeros_like(top), jnp.zeros_like(top)
    for b in range(blocks):
        s = tots[b // nblk, b % nblk, 1]
        o = tots[b // nblk, b % nblk, 2]
        e = jnp.exp2(ms[b] - top)
        ss.append(s * e)
        os.append(o * e)
        e = jnp.where(ms[b] > second, 0.0, jnp.exp2(ms[b] - second))
        s2 = s2 + s * e
        o2 = o2 + o * e
    alone = o2 / s2

    def others(xs):
        fore, back = [jnp.zeros_like(top)], [jnp.zeros_like(top)]
        for b in range(blocks - 1):
            fore.append(fore[-1] + xs[b])
            back.append(back[-1] + xs[blocks - 1 - b])
        back = back[::-1]
        return [fore[b] + back[b] for b in range(blocks)]

    ss, os = others(ss), others(os)
    states_rows = kvh * flat
    for b in range(blocks):
        xs[b * states_rows:(b + 1) * states_rows, :] = jnp.where(ms[b] > second, alone, os[b] / ss[b])
    x = xs[pl.ds(0, blocks, stride=states_rows), :]
    for j in range(1, states_rows):
        x = x + xs[pl.ds(j, blocks, stride=states_rows), :]
    step = nq
    while step < LANES:
        x = x + pltpu.roll(x, step, 1)
        step *= 2
    own[...] = x
    copies = exchange(hn, "heads", own, lambda d: reads.at[d], lambda k: r_send.at[k], lambda k: r_recv.at[k])
    begin(copies)
    reads[mine] = x
    fetch_n.wait()
    finish(copies)
    x = reads[0]
    for k in range(1, hn):
        x = x + reads[k]
    table[...] = x
    read_ref[...] = table[pl.ds(device * nblk, nblk), 0:nq]
    ids = n_v[...]
    picked = jnp.zeros(ids.shape, F32)
    for b in range(blocks):
        picked = jnp.where(ids == b, x[b:b + 1, 0:nq], picked)
    pick_ref[...] = picked


def body(queries, keys, values, out_weight, probe, knocked):
    nq, hq, hd = queries.shape
    kvh = keys.shape[1]
    group = hq // kvh
    nblk = keys.shape[0] // BLOCK
    lanes = lax.axis_size("keys")
    hn = lax.axis_size("heads")
    rows = nq * group
    flat = rows // LANES
    wide = BLOCK * kvh
    piece = min(PIECE, wide)
    blocks = lanes * nblk
    picks = knocked.shape[1]
    dma = pltpu.SemaphoreType.DMA
    vmem = pltpu.VMEM
    hbm = pl.BlockSpec(memory_space=pl.ANY)
    kernel = pl.pallas_call(
        functools.partial(attend, lanes, hn, nblk, kvh, group),
        in_specs=[hbm] * 6,
        out_specs=[pl.BlockSpec(memory_space=pltpu.VMEM)] * 2,
        out_shape=[pltpu.VMEM((nblk, nq), F32), pltpu.VMEM((picks, nq), F32)],
        scratch_shapes=[
            vmem((nq, hq, hd), BF16),
            vmem((nblk * wide, hd), BF16),
            vmem((nblk * wide, hd), BF16),
            vmem(out_weight.shape, BF16),
            vmem((probe.shape[0] // LANES, LANES), BF16),
            vmem((picks, nq), jnp.int32),
            vmem((nq * hq, hd), F32),
            vmem((kvh * hd, rows), BF16),
            vmem((nq * kvh, rows), jnp.int32),
            vmem((2, wide // piece, piece, rows), F32),
            vmem((2, SUBL, rows), F32),
            vmem((3 * hq, hd), BF16),
            vmem((hq, hd), F32),
            vmem((lanes, hq, hd), F32),
            vmem((lanes, nblk, 3, kvh * flat, LANES), F32),
            vmem((blocks * kvh * flat, LANES), F32),
            vmem((blocks, LANES), F32),
            vmem((hn, blocks, LANES), F32),
            vmem((blocks, LANES), F32),
            dma, dma((nblk,)), dma((nblk,)), dma, dma, dma,
            dma((lanes,)), dma((lanes,)), dma((nblk, lanes)), dma((nblk, lanes)), dma((hn,)), dma((hn,)),
        ],
        compiler_params=pltpu.CompilerParams(collective_id=0, has_side_effects=True, vmem_limit_bytes=60 * 2 ** 20),
    )
    readout, picked = kernel(queries, keys.reshape(-1, hd), values.reshape(-1, hd), out_weight,
                             probe.reshape(-1, LANES), knocked.T)
    return (readout.T, picked.T)


def solution(mesh):
    in_specs = (
        P(None, "heads", None),
        P("keys", "heads", None),
        P("keys", "heads", None),
        P("heads", "keys"),
        P("keys"),
        P(),
    )
    out_specs = (P(None, "keys"), P())
    return jax.shard_map(body, mesh=mesh, in_specs=in_specs, out_specs=out_specs, check_vma=False)
```

```python
import functools
import math

import jax
import jax.numpy as jnp
from jax import lax
from jax.experimental import pallas as pl
from jax.experimental.pallas import tpu as pltpu
from jax.sharding import PartitionSpec as P

BLOCK = 4096
NEG = -1e30
LANES = 128
SUBL = 8
PIECE = 2048
STEP = 256
AHEAD = 2
W_PARTS = 2
MESH = pl.DeviceIdType.MESH
F32 = jnp.float32
BF16 = jnp.bfloat16


def exchange(size, axis, src, dst, send, recv):
    me = lax.axis_index(axis)
    out = []
    for k in range(1, size):
        there = lax.rem(me + k, size)
        here = lax.rem(me + size - k, size)
        put = pltpu.make_async_remote_copy(src, dst(me), send(k), recv(k), device_id={axis: there}, device_id_type=MESH)
        get = pltpu.make_async_remote_copy(src, dst(here), send(k), recv(k), device_id={axis: there}, device_id_type=MESH)
        out.append((put, get))
    return out


def begin(copies):
    for put, _ in copies:
        put.start()


def arrive(copies):
    for _, get in copies:
        get.wait_recv()


def leave(copies):
    for put, _ in copies:
        put.wait_send()


def halves(x, parts):
    out = []
    for _ in range(parts - 1):
        out.append(x.astype(BF16))
        x = x - out[-1].astype(F32)
    out.append(x.astype(BF16))
    return out


def attend(lanes, hn, nblk, kvh, group, q_hbm, k_hbm, v_hbm, w_hbm, x_hbm, n_hbm, read_ref, pick_ref,
           q_v, k_v, v_v, w_v, x_v, n_v, qf, qt, rel, sc, tops, dcat, part, dirs, tots, xs, own, reads, table,
           q_s, k_s, v_s, w_s, x_s, n_s, d_send, d_recv, t_send, t_recv, r_send, r_recv):
    nq, hq, hd = q_hbm.shape
    rows = nq * group
    flat = rows // LANES
    per = LANES // nq
    wide = BLOCK * kvh
    piece = min(PIECE, wide)
    blocks = lanes * nblk
    scale = hd ** -0.5 * math.log2(math.e)
    device = lax.axis_index("keys")
    mine = lax.axis_index("heads")
    barrier = pltpu.get_barrier_semaphore()
    for k in range(1, lanes):
        pl.semaphore_signal(barrier, inc=1, device_id={"keys": lax.rem(device + k, lanes)}, device_id_type=MESH)
    for k in range(1, hn):
        pl.semaphore_signal(barrier, inc=1, device_id={"heads": lax.rem(mine + k, hn)}, device_id_type=MESH)

    def part_of(i):
        return pl.ds(pl.multiple_of(i * wide, wide), wide)

    def fetch_k(i):
        return pltpu.make_async_copy(k_hbm.at[part_of(i)], k_v.at[part_of(i)], k_s.at[i])

    def fetch_v(i):
        return pltpu.make_async_copy(v_hbm.at[part_of(i)], v_v.at[part_of(i)], v_s.at[i])

    fetch_q = pltpu.make_async_copy(q_hbm, q_v, q_s)
    w_rows = hq * hd // W_PARTS

    def fetch_w(c):
        return pltpu.make_async_copy(w_hbm.at[pl.ds(c * w_rows, w_rows)], w_v.at[pl.ds(c * w_rows, w_rows)], w_s.at[c])

    fetch_x = pltpu.make_async_copy(x_hbm, x_v, x_s)
    fetch_n = pltpu.make_async_copy(n_hbm, n_v, n_s)
    fetch_q.start()
    fetch_x.start()
    for c in range(W_PARTS):
        fetch_w(c).start()
    fetch_k(0).start()

    tail = nq * kvh
    r = lax.broadcasted_iota(jnp.int32, (tail, rows), 0)
    c = lax.broadcasted_iota(jnp.int32, (tail, rows), 1)
    rel[...] = r // kvh + (BLOCK - nq) - lax.rem(c, nq)
    fetch_q.wait()
    qf[...] = q_v[...].astype(F32).reshape(nq * hq, hd)
    for h in range(kvh):
        for a in range(flat):
            x = jnp.concatenate([qf[pl.ds(h * group + a * per + e, nq, stride=hq), :] for e in range(per)], axis=0)
            qt[h * hd:(h + 1) * hd, a * LANES:(a + 1) * LANES] = x.T.astype(BF16)

    fetch_x.wait()
    x = x_v[...]
    x = jnp.concatenate([x[k:k + 1, :] for k in range(x.shape[0])], axis=1)
    x = jnp.broadcast_to(x, (16, x.shape[1]))
    for c in range(W_PARTS):
        fetch_w(c).wait()
        if c == W_PARTS - 1:
            for i in range(1, min(2, nblk)):
                fetch_k(i).start()
            fetch_v(0).start()
            for i in range(1, nblk):
                if i > 1:
                    fetch_k(i).start()
                fetch_v(i).start()
            fetch_n.start()
        some = lax.dot_general(x, w_v[c * w_rows:(c + 1) * w_rows, :], (((1,), (1,)), ((), ())), preferred_element_type=F32)
        for h in range(w_rows // hd):
            at = c * (w_rows // hd) + h
            part[at:at + 1, :] = some[0:1, h * hd:(h + 1) * hd]
    send_dirs = exchange(lanes, "keys", part, lambda d: dirs.at[d], lambda k: d_send.at[k], lambda k: d_recv.at[k])
    dirs[device] = part[...]

    def states(i):
        return exchange(lanes, "keys", tots.at[device, i], lambda d: tots.at[d, i],
                        lambda k: t_send.at[i, k], lambda k: t_recv.at[i, k])

    odd = lax.broadcasted_iota(jnp.int32, (16, hd), 0)
    pm = [jnp.where(lax.rem(odd, kvh) == h, 1.0, 0.0).astype(BF16)[None] for h in range(kvh)]
    u_row = lax.broadcasted_iota(jnp.int32, (hq, STEP), 0)
    u_col = lax.broadcasted_iota(jnp.int32, (hq, STEP), 1)
    keep = lax.rem(u_col, kvh) == u_row // group
    lane = lax.broadcasted_iota(jnp.int32, (1, LANES), 1)

    def over(op, x):
        step = kvh
        while step < SUBL:
            x = op(x, pltpu.roll(x, step, 0))
            step *= 2
        return x

    def score(i, pieces, m):
        slot = lax.rem(i, 2)
        base = (device * nblk + i) * BLOCK
        first = lanes * nblk * BLOCK - nq
        for t in pieces:
            x = k_v[pl.ds(pl.multiple_of(i * wide + t * piece, piece), piece), :].reshape(piece // 16, 16, hd)
            left = jnp.concatenate([(x * pm[h]).reshape(piece, hd) for h in range(kvh)], axis=1)
            s = jnp.dot(left, qt[...], preferred_element_type=F32) * scale
            if t == wide // piece - 1:
                last = jnp.where(rel[...] <= first - base, s[piece - tail:], NEG)
                s = jnp.concatenate([s[:piece - tail], last], axis=0)
            sc[slot, t] = s
            m = jnp.maximum(m, jnp.max(s.reshape(piece // SUBL, SUBL, rows), axis=0))
        return m

    def project(i, j):
        x = v_v[pl.ds(pl.multiple_of(i * wide + j * STEP, STEP), STEP), :]
        u = lax.dot_general(dcat[...], x, (((1,), (1,)), ((), ())), preferred_element_type=F32)
        u = jnp.where(keep, u[0:hq] + u[hq:2 * hq] + u[2 * hq:3 * hq], 0.0)
        return jnp.concatenate(halves(u, 2), axis=0)

    count = wide // piece
    low = jnp.full((SUBL, rows), 2 * NEG, F32)
    pl.semaphore_wait(barrier, lanes + hn - 2)
    begin(send_dirs)

    @pl.loop(-1, nblk)
    def _(i):
        @pl.when(i < nblk - 1)
        def _():
            fetch_k(i + 1).wait()
            tops[lax.rem(i + 1, 2)] = over(jnp.maximum, score(i + 1, range(count), low))

        @pl.when(i == 0)
        def _():
            arrive(send_dirs)
            direction = dirs[0]
            for k in range(1, lanes):
                direction = direction + dirs[k]
            dcat[...] = jnp.concatenate(halves(direction, 3), axis=0)

        @pl.when(i >= 0)
        def _():
            fetch_v(i).wait()
            slot = lax.rem(i, 2)
            m = tops[slot]
            l = jnp.zeros((SUBL, rows), F32)
            acc = jnp.zeros((2 * hq, rows), F32)
            left = [project(i, j) for j in range(AHEAD)]
            for j in range(wide // STEP):
                if j + AHEAD < wide // STEP:
                    left.append(project(i, j + AHEAD))
                t, g = divmod(j * STEP, piece)
                s = sc[slot, t, g:g + STEP, :]
                p = jnp.exp2(s.reshape(STEP // SUBL, SUBL, rows) - m[None])
                l = l + jnp.sum(p, axis=0)
                acc = acc + jnp.dot(left[j], p.reshape(STEP, rows).astype(BF16), preferred_element_type=F32)
            l = over(jnp.add, l)
            acc = acc[0:hq] + acc[hq:2 * hq]
            for h in range(kvh):
                for a in range(flat):
                    at = slice(a * LANES, (a + 1) * LANES)
                    row = pl.ds(h * flat + a, 1)
                    tots[device, i, 0, row, :] = m[h:h + 1, at]
                    tots[device, i, 1, row, :] = l[h:h + 1, at]
                    o = acc[h * group + a * per:h * group + a * per + 1, at]
                    for e in range(1, per):
                        g = h * group + a * per + e
                        o = jnp.where(lane // nq == e, acc[g:g + 1, at], o)
                    tots[device, i, 2, row, :] = o
            begin(states(i))

    for i in range(nblk):
        arrive(states(i))

    ms = [tots[b // nblk, b % nblk, 0] for b in range(blocks)]
    before, after = [ms[0]], [ms[-1]]
    for b in range(1, blocks):
        before.append(jnp.maximum(before[-1], ms[b]))
        after.append(jnp.maximum(after[-1], ms[blocks - 1 - b]))
    after = after[::-1]
    empty = jnp.full_like(ms[0], NEG)
    rest = [jnp.maximum(before[b - 1] if b else empty, after[b + 1] if b < blocks - 1 else empty) for b in range(blocks)]
    top = before[-1]
    second = functools.reduce(jnp.minimum, rest)
    ss, os, s2, o2 = [], [], jnp.zeros_like(top), jnp.zeros_like(top)
    for b in range(blocks):
        s = tots[b // nblk, b % nblk, 1]
        o = tots[b // nblk, b % nblk, 2]
        e = jnp.exp2(ms[b] - top)
        ss.append(s * e)
        os.append(o * e)
        e = jnp.where(ms[b] > second, 0.0, jnp.exp2(ms[b] - second))
        s2 = s2 + s * e
        o2 = o2 + o * e
    alone = o2 / s2

    def others(xs):
        fore, back = [jnp.zeros_like(top)], [jnp.zeros_like(top)]
        for b in range(blocks - 1):
            fore.append(fore[-1] + xs[b])
            back.append(back[-1] + xs[blocks - 1 - b])
        back = back[::-1]
        return [fore[b] + back[b] for b in range(blocks)]

    ss, os = others(ss), others(os)
    states_rows = kvh * flat
    for b in range(blocks):
        xs[b * states_rows:(b + 1) * states_rows, :] = jnp.where(ms[b] > second, alone, os[b] / ss[b])
    x = xs[pl.ds(0, blocks, stride=states_rows), :]
    for j in range(1, states_rows):
        x = x + xs[pl.ds(j, blocks, stride=states_rows), :]
    step = nq
    while step < LANES:
        x = x + pltpu.roll(x, step, 1)
        step *= 2
    own[...] = x
    copies = exchange(hn, "heads", own, lambda d: reads.at[d], lambda k: r_send.at[k], lambda k: r_recv.at[k])
    begin(copies)
    reads[mine] = x
    fetch_n.wait()
    arrive(copies)
    x = reads[0]
    for k in range(1, hn):
        x = x + reads[k]
    table[...] = x
    read_ref[...] = table[pl.ds(device * nblk, nblk), 0:nq]
    ids = n_v[...]
    picked = jnp.zeros(ids.shape, F32)
    for b in range(blocks):
        picked = jnp.where(ids == b, x[b:b + 1, 0:nq], picked)
    pick_ref[...] = picked
    leave(send_dirs)
    for i in range(nblk):
        leave(states(i))
    leave(copies)


def deliver(read_in, pick_in, read_out, pick_out, sem):
    copies = [pltpu.make_async_copy(read_in, read_out, sem.at[0]), pltpu.make_async_copy(pick_in, pick_out, sem.at[1])]
    for copy in copies:
        copy.start()
    for copy in copies:
        copy.wait()


def body(queries, keys, values, out_weight, probe, knocked):
    nq, hq, hd = queries.shape
    kvh = keys.shape[1]
    group = hq // kvh
    nblk = keys.shape[0] // BLOCK
    lanes = lax.axis_size("keys")
    hn = lax.axis_size("heads")
    rows = nq * group
    flat = rows // LANES
    wide = BLOCK * kvh
    piece = min(PIECE, wide)
    blocks = lanes * nblk
    picks = knocked.shape[1]
    dma = pltpu.SemaphoreType.DMA
    vmem = pltpu.VMEM
    hbm = pl.BlockSpec(memory_space=pl.ANY)
    kernel = pl.pallas_call(
        functools.partial(attend, lanes, hn, nblk, kvh, group),
        in_specs=[hbm] * 6,
        out_specs=[pl.BlockSpec(memory_space=pltpu.VMEM)] * 2,
        out_shape=[pltpu.VMEM((nblk, nq), F32), pltpu.VMEM((picks, nq), F32)],
        scratch_shapes=[
            vmem((nq, hq, hd), BF16),
            vmem((nblk * wide, hd), BF16),
            vmem((nblk * wide, hd), BF16),
            vmem(out_weight.shape, BF16),
            vmem((probe.shape[0] // LANES, LANES), BF16),
            vmem((picks, nq), jnp.int32),
            vmem((nq * hq, hd), F32),
            vmem((kvh * hd, rows), BF16),
            vmem((nq * kvh, rows), jnp.int32),
            vmem((2, wide // piece, piece, rows), F32),
            vmem((2, SUBL, rows), F32),
            vmem((3 * hq, hd), BF16),
            vmem((hq, hd), F32),
            vmem((lanes, hq, hd), F32),
            vmem((lanes, nblk, 3, kvh * flat, LANES), F32),
            vmem((blocks * kvh * flat, LANES), F32),
            vmem((blocks, LANES), F32),
            vmem((hn, blocks, LANES), F32),
            vmem((blocks, LANES), F32),
            dma, dma((nblk,)), dma((nblk,)), dma((W_PARTS,)), dma, dma,
            dma((lanes,)), dma((lanes,)), dma((nblk, lanes)), dma((nblk, lanes)), dma((hn,)), dma((hn,)),
        ],
        compiler_params=pltpu.CompilerParams(collective_id=0, has_side_effects=True, vmem_limit_bytes=60 * 2 ** 20),
    )
    found = kernel(queries, keys.reshape(-1, hd), values.reshape(-1, hd), out_weight,
                             probe.reshape(-1, LANES), knocked.T)
    readout, picked = pl.pallas_call(
        deliver,
        in_specs=[pl.BlockSpec(memory_space=pltpu.VMEM)] * 2,
        out_specs=[hbm] * 2,
        out_shape=[jax.ShapeDtypeStruct(x.shape, F32) for x in found],
        scratch_shapes=[dma((2,))],
    )(*[pltpu.with_memory_space_constraint(x, pltpu.VMEM) for x in found])
    return (readout.T, picked.T)


def solution(mesh):
    in_specs = (
        P(None, "heads", None),
        P("keys", "heads", None),
        P("keys", "heads", None),
        P("heads", "keys"),
        P("keys"),
        P(),
    )
    out_specs = (P(None, "keys"), P())
    return jax.shard_map(body, mesh=mesh, in_specs=in_specs, out_specs=out_specs, check_vma=False)
```

```python
import functools
import math

import jax
import jax.numpy as jnp
from jax import lax
from jax.experimental import pallas as pl
from jax.experimental.pallas import tpu as pltpu
from jax.sharding import PartitionSpec as P

BLOCK = 4096
NEG = -1e30
LANES = 128
SUBL = 8
PIECE = 2048
STEP = 256
AHEAD = 2
W_PARTS = 2
MESH = pl.DeviceIdType.MESH
F32 = jnp.float32
BF16 = jnp.bfloat16


def exchange(size, axis, src, dst, send, recv):
    me = lax.axis_index(axis)
    out = []
    for k in range(1, size):
        there = lax.rem(me + k, size)
        here = lax.rem(me + size - k, size)
        put = pltpu.make_async_remote_copy(src, dst(me), send(k), recv(k), device_id={axis: there}, device_id_type=MESH)
        get = pltpu.make_async_remote_copy(src, dst(here), send(k), recv(k), device_id={axis: there}, device_id_type=MESH)
        out.append((put, get))
    return out


def begin(copies):
    for put, _ in copies:
        put.start()


def arrive(copies):
    for _, get in copies:
        get.wait_recv()


def leave(copies):
    for put, _ in copies:
        put.wait_send()


def halves(x, parts):
    out = []
    for _ in range(parts - 1):
        out.append(x.astype(BF16))
        x = x - out[-1].astype(F32)
    out.append(x.astype(BF16))
    return out


def attend(lanes, hn, nblk, kvh, group, q_hbm, k_hbm, v_hbm, w_hbm, x_hbm, n_hbm, read_ref, pick_ref,
           q_v, k_v, v_v, w_v, x_v, n_v, qf, qt, rel, sc, tops, dcat, part, dirs, tots, xs, own, reads, table,
           q_s, k_s, v_s, w_s, x_s, n_s, d_send, d_recv, t_send, t_recv, r_send, r_recv):
    nq, hq, hd = q_hbm.shape
    rows = nq * group
    flat = rows // LANES
    per = LANES // nq
    wide = BLOCK * kvh
    piece = min(PIECE, wide)
    blocks = lanes * nblk
    scale = hd ** -0.5 * math.log2(math.e)
    device = lax.axis_index("keys")
    mine = lax.axis_index("heads")
    barrier = pltpu.get_barrier_semaphore()
    for k in range(1, lanes):
        pl.semaphore_signal(barrier, inc=1, device_id={"keys": lax.rem(device + k, lanes)}, device_id_type=MESH)
    for k in range(1, hn):
        pl.semaphore_signal(barrier, inc=1, device_id={"heads": lax.rem(mine + k, hn)}, device_id_type=MESH)

    def part_of(i):
        return pl.ds(pl.multiple_of(i * wide, wide), wide)

    def fetch_k(i):
        return pltpu.make_async_copy(k_hbm.at[part_of(i)], k_v.at[part_of(i)], k_s.at[i])

    def fetch_v(i):
        return pltpu.make_async_copy(v_hbm.at[part_of(i)], v_v.at[part_of(i)], v_s.at[i])

    fetch_q = pltpu.make_async_copy(q_hbm, q_v, q_s)
    w_rows = hq * hd // W_PARTS

    def fetch_w(c):
        return pltpu.make_async_copy(w_hbm.at[pl.ds(c * w_rows, w_rows)], w_v.at[pl.ds(c * w_rows, w_rows)], w_s.at[c])

    fetch_x = pltpu.make_async_copy(x_hbm, x_v, x_s)
    fetch_n = pltpu.make_async_copy(n_hbm, n_v, n_s)
    fetch_q.start()
    fetch_x.start()
    for c in range(W_PARTS):
        fetch_w(c).start()
    fetch_k(0).start()

    tail = nq * kvh
    r = lax.broadcasted_iota(jnp.int32, (tail, rows), 0)
    c = lax.broadcasted_iota(jnp.int32, (tail, rows), 1)
    rel[...] = r // kvh + (BLOCK - nq) - lax.rem(c, nq)
    fetch_q.wait()
    qf[...] = q_v[...].astype(F32).reshape(nq * hq, hd)
    for h in range(kvh):
        for a in range(flat):
            x = jnp.concatenate([qf[pl.ds(h * group + a * per + e, nq, stride=hq), :] for e in range(per)], axis=0)
            qt[h * hd:(h + 1) * hd, a * LANES:(a + 1) * LANES] = x.T.astype(BF16)

    fetch_x.wait()
    x = x_v[...]
    x = jnp.concatenate([x[k:k + 1, :] for k in range(x.shape[0])], axis=1)
    x = jnp.broadcast_to(x, (16, x.shape[1]))
    for c in range(W_PARTS):
        fetch_w(c).wait()
        if c == W_PARTS - 1:
            for i in range(1, min(2, nblk)):
                fetch_k(i).start()
            fetch_v(0).start()
            for i in range(1, nblk):
                if i > 1:
                    fetch_k(i).start()
                fetch_v(i).start()
            fetch_n.start()
        some = lax.dot_general(x, w_v[c * w_rows:(c + 1) * w_rows, :], (((1,), (1,)), ((), ())), preferred_element_type=F32)
        for h in range(w_rows // hd):
            at = c * (w_rows // hd) + h
            part[at:at + 1, :] = some[0:1, h * hd:(h + 1) * hd]
    send_dirs = exchange(lanes, "keys", part, lambda d: dirs.at[d], lambda k: d_send.at[k], lambda k: d_recv.at[k])
    dirs[device] = part[...]

    def states(i):
        return exchange(lanes, "keys", tots.at[device, i], lambda d: tots.at[d, i],
                        lambda k: t_send.at[i, k], lambda k: t_recv.at[i, k])

    odd = lax.broadcasted_iota(jnp.int32, (16, hd), 0)
    pm = [jnp.where(lax.rem(odd, kvh) == h, 1.0, 0.0).astype(BF16)[None] for h in range(kvh)]
    u_row = lax.broadcasted_iota(jnp.int32, (hq, STEP), 0)
    u_col = lax.broadcasted_iota(jnp.int32, (hq, STEP), 1)
    keep = lax.rem(u_col, kvh) == u_row // group
    lane = lax.broadcasted_iota(jnp.int32, (1, LANES), 1)

    def over(op, x):
        step = kvh
        while step < SUBL:
            x = op(x, pltpu.roll(x, step, 0))
            step *= 2
        return x

    def score(i, pieces, m):
        slot = lax.rem(i, 2)
        base = (device * nblk + i) * BLOCK
        first = lanes * nblk * BLOCK - nq
        for t in pieces:
            x = k_v[pl.ds(pl.multiple_of(i * wide + t * piece, piece), piece), :].reshape(piece // 16, 16, hd)
            left = jnp.concatenate([(x * pm[h]).reshape(piece, hd) for h in range(kvh)], axis=1)
            s = jnp.dot(left, qt[...], preferred_element_type=F32) * scale
            if t == wide // piece - 1:
                last = jnp.where(rel[...] <= first - base, s[piece - tail:], NEG)
                s = jnp.concatenate([s[:piece - tail], last], axis=0)
            sc[slot, t] = s
            m = jnp.maximum(m, jnp.max(s.reshape(piece // SUBL, SUBL, rows), axis=0))
        return m

    def project(i, j):
        x = v_v[pl.ds(pl.multiple_of(i * wide + j * STEP, STEP), STEP), :]
        u = lax.dot_general(dcat[...], x, (((1,), (1,)), ((), ())), preferred_element_type=F32)
        u = jnp.where(keep, u[0:hq] + u[hq:2 * hq] + u[2 * hq:3 * hq], 0.0)
        return jnp.concatenate(halves(u, 2), axis=0)

    count = wide // piece
    low = jnp.full((SUBL, rows), 2 * NEG, F32)
    pl.semaphore_wait(barrier, lanes + hn - 2)
    begin(send_dirs)

    ahead = min(2, nblk)

    @pl.loop(0, ahead)
    def _(i):
        fetch_k(i).wait()
        tops[i] = over(jnp.maximum, score(i, range(count), low))

    arrive(send_dirs)
    direction = dirs[0]
    for k in range(1, lanes):
        direction = direction + dirs[k]
    dcat[...] = jnp.concatenate(halves(direction, 3), axis=0)

    def weigh(i):
        slot = lax.rem(i, 2)
        m = tops[slot]
        l = jnp.zeros((SUBL, rows), F32)
        acc = jnp.zeros((2 * hq, rows), F32)
        left = [project(i, j) for j in range(AHEAD)]
        for j in range(wide // STEP):
            if j + AHEAD < wide // STEP:
                left.append(project(i, j + AHEAD))
            t, g = divmod(j * STEP, piece)
            s = sc[slot, t, g:g + STEP, :]
            p = jnp.exp2(s.reshape(STEP // SUBL, SUBL, rows) - m[None])
            l = l + jnp.sum(p, axis=0)
            acc = acc + jnp.dot(left[j], p.reshape(STEP, rows).astype(BF16), preferred_element_type=F32)
        l = over(jnp.add, l)
        acc = acc[0:hq] + acc[hq:2 * hq]
        for h in range(kvh):
            for a in range(flat):
                at = slice(a * LANES, (a + 1) * LANES)
                row = pl.ds(h * flat + a, 1)
                tots[device, i, 0, row, :] = m[h:h + 1, at]
                tots[device, i, 1, row, :] = l[h:h + 1, at]
                o = acc[h * group + a * per:h * group + a * per + 1, at]
                for e in range(1, per):
                    g = h * group + a * per + e
                    o = jnp.where(lane // nq == e, acc[g:g + 1, at], o)
                tots[device, i, 2, row, :] = o

    @pl.loop(0, nblk - ahead)
    def _(i):
        fetch_v(i).wait()
        fetch_k(i + ahead).wait()
        weigh(i)
        tops[lax.rem(i, 2)] = over(jnp.maximum, score(i + ahead, range(count), low))
        begin(states(i))

    @pl.loop(nblk - ahead, nblk)
    def _(i):
        fetch_v(i).wait()
        weigh(i)
        begin(states(i))

    for i in range(nblk):
        arrive(states(i))

    ms = [tots[b // nblk, b % nblk, 0] for b in range(blocks)]
    before, after = [ms[0]], [ms[-1]]
    for b in range(1, blocks):
        before.append(jnp.maximum(before[-1], ms[b]))
        after.append(jnp.maximum(after[-1], ms[blocks - 1 - b]))
    after = after[::-1]
    empty = jnp.full_like(ms[0], NEG)
    rest = [jnp.maximum(before[b - 1] if b else empty, after[b + 1] if b < blocks - 1 else empty) for b in range(blocks)]
    top = before[-1]
    second = functools.reduce(jnp.minimum, rest)
    ss, os, s2, o2 = [], [], jnp.zeros_like(top), jnp.zeros_like(top)
    for b in range(blocks):
        s = tots[b // nblk, b % nblk, 1]
        o = tots[b // nblk, b % nblk, 2]
        e = jnp.exp2(ms[b] - top)
        ss.append(s * e)
        os.append(o * e)
        e = jnp.where(ms[b] > second, 0.0, jnp.exp2(ms[b] - second))
        s2 = s2 + s * e
        o2 = o2 + o * e
    alone = o2 / s2

    def others(xs):
        fore, back = [jnp.zeros_like(top)], [jnp.zeros_like(top)]
        for b in range(blocks - 1):
            fore.append(fore[-1] + xs[b])
            back.append(back[-1] + xs[blocks - 1 - b])
        back = back[::-1]
        return [fore[b] + back[b] for b in range(blocks)]

    ss, os = others(ss), others(os)
    states_rows = kvh * flat
    for b in range(blocks):
        xs[b * states_rows:(b + 1) * states_rows, :] = jnp.where(ms[b] > second, alone, os[b] / ss[b])
    x = xs[pl.ds(0, blocks, stride=states_rows), :]
    for j in range(1, states_rows):
        x = x + xs[pl.ds(j, blocks, stride=states_rows), :]
    step = nq
    while step < LANES:
        x = x + pltpu.roll(x, step, 1)
        step *= 2
    own[...] = x
    copies = exchange(hn, "heads", own, lambda d: reads.at[d], lambda k: r_send.at[k], lambda k: r_recv.at[k])
    begin(copies)
    reads[mine] = x
    fetch_n.wait()
    arrive(copies)
    x = reads[0]
    for k in range(1, hn):
        x = x + reads[k]
    table[...] = x
    read_ref[...] = table[pl.ds(device * nblk, nblk), 0:nq]
    ids = n_v[...]
    picked = jnp.zeros(ids.shape, F32)
    for b in range(blocks):
        picked = jnp.where(ids == b, x[b:b + 1, 0:nq], picked)
    pick_ref[...] = picked
    leave(send_dirs)
    for i in range(nblk):
        leave(states(i))
    leave(copies)


def deliver(read_in, pick_in, read_out, pick_out, sem):
    copies = [pltpu.make_async_copy(read_in, read_out, sem.at[0]), pltpu.make_async_copy(pick_in, pick_out, sem.at[1])]
    for copy in copies:
        copy.start()
    for copy in copies:
        copy.wait()


def body(queries, keys, values, out_weight, probe, knocked):
    nq, hq, hd = queries.shape
    kvh = keys.shape[1]
    group = hq // kvh
    nblk = keys.shape[0] // BLOCK
    lanes = lax.axis_size("keys")
    hn = lax.axis_size("heads")
    rows = nq * group
    flat = rows // LANES
    wide = BLOCK * kvh
    piece = min(PIECE, wide)
    blocks = lanes * nblk
    picks = knocked.shape[1]
    dma = pltpu.SemaphoreType.DMA
    vmem = pltpu.VMEM
    hbm = pl.BlockSpec(memory_space=pl.ANY)
    kernel = pl.pallas_call(
        functools.partial(attend, lanes, hn, nblk, kvh, group),
        in_specs=[hbm] * 6,
        out_specs=[pl.BlockSpec(memory_space=pltpu.VMEM)] * 2,
        out_shape=[pltpu.VMEM((nblk, nq), F32), pltpu.VMEM((picks, nq), F32)],
        scratch_shapes=[
            vmem((nq, hq, hd), BF16),
            vmem((nblk * wide, hd), BF16),
            vmem((nblk * wide, hd), BF16),
            vmem(out_weight.shape, BF16),
            vmem((probe.shape[0] // LANES, LANES), BF16),
            vmem((picks, nq), jnp.int32),
            vmem((nq * hq, hd), F32),
            vmem((kvh * hd, rows), BF16),
            vmem((nq * kvh, rows), jnp.int32),
            vmem((2, wide // piece, piece, rows), F32),
            vmem((2, SUBL, rows), F32),
            vmem((3 * hq, hd), BF16),
            vmem((hq, hd), F32),
            vmem((lanes, hq, hd), F32),
            vmem((lanes, nblk, 3, kvh * flat, LANES), F32),
            vmem((blocks * kvh * flat, LANES), F32),
            vmem((blocks, LANES), F32),
            vmem((hn, blocks, LANES), F32),
            vmem((blocks, LANES), F32),
            dma, dma((nblk,)), dma((nblk,)), dma((W_PARTS,)), dma, dma,
            dma((lanes,)), dma((lanes,)), dma((nblk, lanes)), dma((nblk, lanes)), dma((hn,)), dma((hn,)),
        ],
        compiler_params=pltpu.CompilerParams(collective_id=0, has_side_effects=True, vmem_limit_bytes=60 * 2 ** 20),
    )
    found = kernel(queries, keys.reshape(-1, hd), values.reshape(-1, hd), out_weight,
                             probe.reshape(-1, LANES), knocked.T)
    readout, picked = pl.pallas_call(
        deliver,
        in_specs=[pl.BlockSpec(memory_space=pltpu.VMEM)] * 2,
        out_specs=[hbm] * 2,
        out_shape=[jax.ShapeDtypeStruct(x.shape, F32) for x in found],
        scratch_shapes=[dma((2,))],
    )(*[pltpu.with_memory_space_constraint(x, pltpu.VMEM) for x in found])
    return (readout.T, picked.T)


def solution(mesh):
    in_specs = (
        P(None, "heads", None),
        P("keys", "heads", None),
        P("keys", "heads", None),
        P("heads", "keys"),
        P("keys"),
        P(),
    )
    out_specs = (P(None, "keys"), P())
    return jax.shard_map(body, mesh=mesh, in_specs=in_specs, out_specs=out_specs, check_vma=False)
```

```python
import functools
import math

import jax
import jax.numpy as jnp
from jax import lax
from jax.experimental import pallas as pl
from jax.experimental.pallas import tpu as pltpu
from jax.sharding import PartitionSpec as P

BLOCK = 4096
NEG = -1e30
LANES = 128
SUBL = 8
PIECE = 2048
STEP = 256
AHEAD = 2
W_PARTS = 2
MESH = pl.DeviceIdType.MESH
F32 = jnp.float32
BF16 = jnp.bfloat16


def exchange(size, axis, src, dst, send, recv):
    me = lax.axis_index(axis)
    out = []
    for k in range(1, size):
        low = k - 1 + jnp.where(k - 1 >= me, 1, 0)
        high = size - k - jnp.where(size - k <= me, 1, 0)
        there = jnp.where(me < size // 2, high, low)
        put = pltpu.make_async_remote_copy(src, dst(me), send(k), recv(me), device_id={axis: there}, device_id_type=MESH)
        get = pltpu.make_async_remote_copy(src, dst(there), send(k), recv(there), device_id={axis: there}, device_id_type=MESH)
        out.append((put, get))
    return out


def begin(copies):
    for put, _ in copies:
        put.start()


def arrive(copies):
    for _, get in copies:
        get.wait_recv()


def leave(copies):
    for put, _ in copies:
        put.wait_send()


def halves(x, parts):
    out = []
    for _ in range(parts - 1):
        out.append(x.astype(BF16))
        x = x - out[-1].astype(F32)
    out.append(x.astype(BF16))
    return out


def attend(lanes, hn, nblk, kvh, group, q_hbm, k_hbm, v_hbm, w_hbm, x_hbm, n_hbm, read_ref, pick_ref,
           q_v, k_v, v_v, w_v, x_v, n_v, qf, qt, rel, sc, tops, dcat, part, dirs, tots, xs, own, reads, table,
           q_s, k_s, v_s, w_s, x_s, n_s, d_send, d_recv, t_send, t_recv, r_send, r_recv):
    nq, hq, hd = q_hbm.shape
    rows = nq * group
    flat = rows // LANES
    per = LANES // nq
    wide = BLOCK * kvh
    piece = min(PIECE, wide)
    blocks = lanes * nblk
    scale = hd ** -0.5 * math.log2(math.e)
    device = lax.axis_index("keys")
    mine = lax.axis_index("heads")
    barrier = pltpu.get_barrier_semaphore()
    for k in range(1, lanes):
        pl.semaphore_signal(barrier, inc=1, device_id={"keys": lax.rem(device + k, lanes)}, device_id_type=MESH)
    for k in range(1, hn):
        pl.semaphore_signal(barrier, inc=1, device_id={"heads": lax.rem(mine + k, hn)}, device_id_type=MESH)

    def part_of(i):
        return pl.ds(pl.multiple_of(i * wide, wide), wide)

    def fetch_k(i):
        return pltpu.make_async_copy(k_hbm.at[part_of(i)], k_v.at[part_of(i)], k_s.at[i])

    def fetch_v(i):
        return pltpu.make_async_copy(v_hbm.at[part_of(i)], v_v.at[part_of(i)], v_s.at[i])

    fetch_q = pltpu.make_async_copy(q_hbm, q_v, q_s)
    w_rows = hq * hd // W_PARTS

    def fetch_w(c):
        return pltpu.make_async_copy(w_hbm.at[pl.ds(c * w_rows, w_rows)], w_v.at[pl.ds(c * w_rows, w_rows)], w_s.at[c])

    fetch_x = pltpu.make_async_copy(x_hbm, x_v, x_s)
    fetch_n = pltpu.make_async_copy(n_hbm, n_v, n_s)
    fetch_q.start()
    fetch_x.start()
    for c in range(W_PARTS):
        fetch_w(c).start()
    fetch_k(0).start()

    tail = nq * kvh
    r = lax.broadcasted_iota(jnp.int32, (tail, rows), 0)
    c = lax.broadcasted_iota(jnp.int32, (tail, rows), 1)
    rel[...] = r // kvh + (BLOCK - nq) - lax.rem(c, nq)
    fetch_q.wait()
    qf[...] = q_v[...].astype(F32).reshape(nq * hq, hd)
    for h in range(kvh):
        for a in range(flat):
            x = jnp.concatenate([qf[pl.ds(h * group + a * per + e, nq, stride=hq), :] for e in range(per)], axis=0)
            qt[h * hd:(h + 1) * hd, a * LANES:(a + 1) * LANES] = x.T.astype(BF16)

    fetch_x.wait()
    x = x_v[...]
    x = jnp.concatenate([x[k:k + 1, :] for k in range(x.shape[0])], axis=1)
    x = jnp.broadcast_to(x, (16, x.shape[1]))
    for c in range(W_PARTS):
        fetch_w(c).wait()
        if c == W_PARTS - 1:
            for i in range(1, min(2, nblk)):
                fetch_k(i).start()
            fetch_v(0).start()
            for i in range(1, nblk):
                if i > 1:
                    fetch_k(i).start()
                fetch_v(i).start()
            fetch_n.start()
        some = lax.dot_general(x, w_v[c * w_rows:(c + 1) * w_rows, :], (((1,), (1,)), ((), ())), preferred_element_type=F32)
        for h in range(w_rows // hd):
            at = c * (w_rows // hd) + h
            part[at:at + 1, :] = some[0:1, h * hd:(h + 1) * hd]
    send_dirs = exchange(lanes, "keys", part, lambda d: dirs.at[d], lambda k: d_send.at[k], lambda k: d_recv.at[k])
    dirs[device] = part[...]

    def states(i):
        return exchange(lanes, "keys", tots.at[device, i], lambda d: tots.at[d, i],
                        lambda k: t_send.at[i, k], lambda k: t_recv.at[i, k])

    odd = lax.broadcasted_iota(jnp.int32, (16, hd), 0)
    pm = [jnp.where(lax.rem(odd, kvh) == h, 1.0, 0.0).astype(BF16)[None] for h in range(kvh)]
    u_row = lax.broadcasted_iota(jnp.int32, (hq, STEP), 0)
    u_col = lax.broadcasted_iota(jnp.int32, (hq, STEP), 1)
    keep = lax.rem(u_col, kvh) == u_row // group
    lane = lax.broadcasted_iota(jnp.int32, (1, LANES), 1)

    def over(op, x):
        step = kvh
        while step < SUBL:
            x = op(x, pltpu.roll(x, step, 0))
            step *= 2
        return x

    def score(i, pieces, m):
        slot = lax.rem(i, 2)
        base = (device * nblk + i) * BLOCK
        first = lanes * nblk * BLOCK - nq
        for t in pieces:
            x = k_v[pl.ds(pl.multiple_of(i * wide + t * piece, piece), piece), :].reshape(piece // 16, 16, hd)
            left = jnp.concatenate([(x * pm[h]).reshape(piece, hd) for h in range(kvh)], axis=1)
            s = jnp.dot(left, qt[...], preferred_element_type=F32) * scale
            if t == wide // piece - 1:
                last = jnp.where(rel[...] <= first - base, s[piece - tail:], NEG)
                s = jnp.concatenate([s[:piece - tail], last], axis=0)
            sc[slot, t] = s
            m = jnp.maximum(m, jnp.max(s.reshape(piece // SUBL, SUBL, rows), axis=0))
        return m

    def project(i, j):
        x = v_v[pl.ds(pl.multiple_of(i * wide + j * STEP, STEP), STEP), :]
        u = lax.dot_general(dcat[...], x, (((1,), (1,)), ((), ())), preferred_element_type=F32)
        u = jnp.where(keep, u[0:hq] + u[hq:2 * hq] + u[2 * hq:3 * hq], 0.0)
        return jnp.concatenate(halves(u, 2), axis=0)

    count = wide // piece
    low = jnp.full((SUBL, rows), 2 * NEG, F32)
    pl.semaphore_wait(barrier, lanes + hn - 2)
    begin(send_dirs)

    ahead = min(2, nblk)

    @pl.loop(0, ahead)
    def _(i):
        fetch_k(i).wait()
        tops[i] = over(jnp.maximum, score(i, range(count), low))

    arrive(send_dirs)
    direction = dirs[0]
    for k in range(1, lanes):
        direction = direction + dirs[k]
    dcat[...] = jnp.concatenate(halves(direction, 3), axis=0)

    def weigh(i):
        slot = lax.rem(i, 2)
        m = tops[slot]
        l = jnp.zeros((SUBL, rows), F32)
        acc = jnp.zeros((2 * hq, rows), F32)
        left = [project(i, j) for j in range(AHEAD)]
        for j in range(wide // STEP):
            if j + AHEAD < wide // STEP:
                left.append(project(i, j + AHEAD))
            t, g = divmod(j * STEP, piece)
            s = sc[slot, t, g:g + STEP, :]
            p = jnp.exp2(s.reshape(STEP // SUBL, SUBL, rows) - m[None])
            l = l + jnp.sum(p, axis=0)
            acc = acc + jnp.dot(left[j], p.reshape(STEP, rows).astype(BF16), preferred_element_type=F32)
        l = over(jnp.add, l)
        acc = acc[0:hq] + acc[hq:2 * hq]
        for h in range(kvh):
            for a in range(flat):
                at = slice(a * LANES, (a + 1) * LANES)
                row = pl.ds(h * flat + a, 1)
                tots[device, i, 0, row, :] = m[h:h + 1, at]
                tots[device, i, 1, row, :] = l[h:h + 1, at]
                o = acc[h * group + a * per:h * group + a * per + 1, at]
                for e in range(1, per):
                    g = h * group + a * per + e
                    o = jnp.where(lane // nq == e, acc[g:g + 1, at], o)
                tots[device, i, 2, row, :] = o

    @pl.loop(0, nblk - ahead)
    def _(i):
        fetch_v(i).wait()
        fetch_k(i + ahead).wait()
        weigh(i)
        tops[lax.rem(i, 2)] = over(jnp.maximum, score(i + ahead, range(count), low))
        begin(states(i))

    @pl.loop(nblk - ahead, nblk)
    def _(i):
        fetch_v(i).wait()
        weigh(i)
        begin(states(i))

    for i in range(nblk):
        arrive(states(i))

    ms = [tots[b // nblk, b % nblk, 0] for b in range(blocks)]
    before, after = [ms[0]], [ms[-1]]
    for b in range(1, blocks):
        before.append(jnp.maximum(before[-1], ms[b]))
        after.append(jnp.maximum(after[-1], ms[blocks - 1 - b]))
    after = after[::-1]
    empty = jnp.full_like(ms[0], NEG)
    rest = [jnp.maximum(before[b - 1] if b else empty, after[b + 1] if b < blocks - 1 else empty) for b in range(blocks)]
    top = before[-1]
    second = functools.reduce(jnp.minimum, rest)
    ss, os, s2, o2 = [], [], jnp.zeros_like(top), jnp.zeros_like(top)
    for b in range(blocks):
        s = tots[b // nblk, b % nblk, 1]
        o = tots[b // nblk, b % nblk, 2]
        e = jnp.exp2(ms[b] - top)
        ss.append(s * e)
        os.append(o * e)
        e = jnp.where(ms[b] > second, 0.0, jnp.exp2(ms[b] - second))
        s2 = s2 + s * e
        o2 = o2 + o * e
    alone = o2 / s2

    def others(xs):
        fore, back = [jnp.zeros_like(top)], [jnp.zeros_like(top)]
        for b in range(blocks - 1):
            fore.append(fore[-1] + xs[b])
            back.append(back[-1] + xs[blocks - 1 - b])
        back = back[::-1]
        return [fore[b] + back[b] for b in range(blocks)]

    ss, os = others(ss), others(os)
    states_rows = kvh * flat
    for b in range(blocks):
        xs[b * states_rows:(b + 1) * states_rows, :] = jnp.where(ms[b] > second, alone, os[b] / ss[b])
    x = xs[pl.ds(0, blocks, stride=states_rows), :]
    for j in range(1, states_rows):
        x = x + xs[pl.ds(j, blocks, stride=states_rows), :]
    step = nq
    while step < LANES:
        x = x + pltpu.roll(x, step, 1)
        step *= 2
    own[...] = x
    copies = exchange(hn, "heads", own, lambda d: reads.at[d], lambda k: r_send.at[k], lambda k: r_recv.at[k])
    begin(copies)
    reads[mine] = x
    fetch_n.wait()
    arrive(copies)
    x = reads[0]
    for k in range(1, hn):
        x = x + reads[k]
    table[...] = x
    read_ref[...] = table[pl.ds(device * nblk, nblk), 0:nq]
    ids = n_v[...]
    picked = jnp.zeros(ids.shape, F32)
    for b in range(blocks):
        picked = jnp.where(ids == b, x[b:b + 1, 0:nq], picked)
    pick_ref[...] = picked
    leave(send_dirs)
    for i in range(nblk):
        leave(states(i))
    leave(copies)


def deliver(read_in, pick_in, read_out, pick_out, sem):
    copies = [pltpu.make_async_copy(read_in, read_out, sem.at[0]), pltpu.make_async_copy(pick_in, pick_out, sem.at[1])]
    for copy in copies:
        copy.start()
    for copy in copies:
        copy.wait()


def body(queries, keys, values, out_weight, probe, knocked):
    nq, hq, hd = queries.shape
    kvh = keys.shape[1]
    group = hq // kvh
    nblk = keys.shape[0] // BLOCK
    lanes = lax.axis_size("keys")
    hn = lax.axis_size("heads")
    rows = nq * group
    flat = rows // LANES
    wide = BLOCK * kvh
    piece = min(PIECE, wide)
    blocks = lanes * nblk
    picks = knocked.shape[1]
    dma = pltpu.SemaphoreType.DMA
    vmem = pltpu.VMEM
    hbm = pl.BlockSpec(memory_space=pl.ANY)
    kernel = pl.pallas_call(
        functools.partial(attend, lanes, hn, nblk, kvh, group),
        in_specs=[hbm] * 6,
        out_specs=[pl.BlockSpec(memory_space=pltpu.VMEM)] * 2,
        out_shape=[pltpu.VMEM((nblk, nq), F32), pltpu.VMEM((picks, nq), F32)],
        scratch_shapes=[
            vmem((nq, hq, hd), BF16),
            vmem((nblk * wide, hd), BF16),
            vmem((nblk * wide, hd), BF16),
            vmem(out_weight.shape, BF16),
            vmem((probe.shape[0] // LANES, LANES), BF16),
            vmem((picks, nq), jnp.int32),
            vmem((nq * hq, hd), F32),
            vmem((kvh * hd, rows), BF16),
            vmem((nq * kvh, rows), jnp.int32),
            vmem((2, wide // piece, piece, rows), F32),
            vmem((2, SUBL, rows), F32),
            vmem((3 * hq, hd), BF16),
            vmem((hq, hd), F32),
            vmem((lanes, hq, hd), F32),
            vmem((lanes, nblk, 3, kvh * flat, LANES), F32),
            vmem((blocks * kvh * flat, LANES), F32),
            vmem((blocks, LANES), F32),
            vmem((hn, blocks, LANES), F32),
            vmem((blocks, LANES), F32),
            dma, dma((nblk,)), dma((nblk,)), dma((W_PARTS,)), dma, dma,
            dma((lanes,)), dma((lanes,)), dma((nblk, lanes)), dma((nblk, lanes)), dma((hn,)), dma((hn,)),
        ],
        compiler_params=pltpu.CompilerParams(collective_id=0, has_side_effects=True, vmem_limit_bytes=60 * 2 ** 20),
    )
    found = kernel(queries, keys.reshape(-1, hd), values.reshape(-1, hd), out_weight,
                             probe.reshape(-1, LANES), knocked.T)
    readout, picked = pl.pallas_call(
        deliver,
        in_specs=[pl.BlockSpec(memory_space=pltpu.VMEM)] * 2,
        out_specs=[hbm] * 2,
        out_shape=[jax.ShapeDtypeStruct(x.shape, F32) for x in found],
        scratch_shapes=[dma((2,))],
    )(*[pltpu.with_memory_space_constraint(x, pltpu.VMEM) for x in found])
    return (readout.T, picked.T)


def solution(mesh):
    in_specs = (
        P(None, "heads", None),
        P("keys", "heads", None),
        P("keys", "heads", None),
        P("heads", "keys"),
        P("keys"),
        P(),
    )
    out_specs = (P(None, "keys"), P())
    return jax.shard_map(body, mesh=mesh, in_specs=in_specs, out_specs=out_specs, check_vma=False)
```
